256 devices in a mesh: req: 32 (over z, y), tp: 8 (over x, core).
Axes of the slice: x: 4, y: 4, z: 8, core: 2. Of those that a mesh axis runs over, the one named last changes fastest.
Arguments:
- hidden: bfloat16 [9472, 5120], P('req', 'tp'), may hold values from -6 to 6
- raw_q: bfloat16 [9472, 3072], P('req', 'tp'), may hold values from -70 to 70
- raw_k: bfloat16 [9472, 3072], P('req', 'tp'), may hold values from -70 to 70
- raw_v: bfloat16 [9472, 3072], P('req', 'tp'), may hold values from -6 to 6
- q_gain: float32 [3072], P('tp'), may hold values from 0.5 to 2
- k_gain: float32 [3072], P('tp'), may hold values from 0.5 to 2
- out_weight: bfloat16 [3072, 5120], P('tp'), may hold values from -0.109375 to 0.109375
- post_gain: float32 [5120], P('tp'), may hold values from 0.25 to 1.75
- prefix_keys: bfloat16 [32, 32, 128, 3072], P(None, 'req', None, 'tp'), may hold values from -420 to 420
- prefix_values: bfloat16 [32, 32, 128, 3072], P(None, 'req', None, 'tp'), may hold values from -6 to 6
- key_cache: bfloat16 [256, 128, 3072], P('req', None, 'tp'), may hold values from -420 to 420
- value_cache: bfloat16 [256, 128, 3072], P('req', None, 'tp'), may hold values from -6 to 6
- slot_owner: int32 [256], P('req'), may hold values from -1 to 255, as said below
- slot_page: int32 [256], P('req'), may hold values from 0 to 127, as said below
- cache_lengths: int32 [256], replicated, may hold values from 0 to 16384, as said below
- span_offsets: int32 [32], replicated, may hold values from 0 to 4096
Outputs:
- new_hidden: bfloat16 [9472, 5120], P('req', 'tp')
The draws below stay inside these ranges and needn't reach their ends.
Inputs may be any that keep to these rules, and one draw needn't show every extreme that they name: Each pool slot holds one page of decode request slot_owner[s], or nothing where it is -1. No page of a request is held twice, and a request holding c pages holds pages 0 to c - 1. `slot_page`: 0 for a slot that holds nothing. `cache_lengths`: A request holding c pages of the pool has a length from (c - 1) * 128 + 1 to c * 128, and 0 where c = 0.
All inputs are finite; a program needn't handle non-finite values.
Results may differ from the reference program's by a relative error of at most 0.0076.
Values may be sent and summed in bfloat16 or wider, within the bound.
A program may use at most 128 MiB of HBM per device.

```python
import math
import jax
import jax.numpy as jnp
from jax import lax

D = 5120
HEADS = 24
HD = 128
PAGE = 128
SPAN = 288
DEC = 8
GROUPS = 32
REQUESTS = 256
ROWS = 9472
PRE_PAGES = 32
POOL = 256
LEN_PAGES = 128


def cache_keys(key, salt, lead_shape):
    shape = lead_shape + (PAGE, HEADS * HD)
    noise_key = jax.random.fold_in(key, salt + 100)
    return jnp.clip(jax.random.normal(noise_key, shape, jnp.float32), -6.0, 6.0).astype(jnp.bfloat16)


def cache_values(key, salt, lead_shape):
    shape = lead_shape + (PAGE, HEADS * HD)
    noise_key = jax.random.fold_in(key, salt + 200)
    return jnp.clip(jax.random.normal(noise_key, shape, jnp.float32), -6.0, 6.0).astype(jnp.bfloat16)


def rising_features(key, salt):
    width = HEADS * HD
    noise_key = jax.random.fold_in(key, salt)
    column = jnp.arange(width, dtype=jnp.float32) / (width - 1)
    base_values = jnp.clip(jax.random.normal(noise_key, (ROWS, width), jnp.float32), -6.0, 6.0)
    return (base_values * jnp.exp(column * 2.3025851)[None, :]).astype(jnp.bfloat16)


def allocate(key):
    subkeys = jax.random.split(key, 6)
    chosen = jax.random.randint(subkeys[0], (), 0, REQUESTS)
    bounds = jax.random.randint(subkeys[1], (POOL,), 1, REQUESTS + 1)
    picked = jax.random.randint(subkeys[2], (POOL,), 0, bounds)
    relabel = jax.random.permutation(subkeys[3], REQUESTS)
    owners = relabel[picked]
    slot_order = jnp.arange(POOL, dtype=jnp.int32)
    owners = jnp.where(slot_order < LEN_PAGES, chosen, owners)
    owners = jnp.where(slot_order == POOL - 1, -1, owners)
    request_ids = jnp.arange(REQUESTS, dtype=jnp.int32)
    onehot = (owners[:, None] == request_ids[None, :]).astype(jnp.int32)
    before = jnp.cumsum(onehot, 0) - onehot
    page_rank = jnp.sum(before * onehot, 1)
    owners = jnp.where(page_rank < LEN_PAGES, owners, -1)
    page_rank = jnp.where(owners >= 0, page_rank, 0)
    counts = jnp.sum((owners[:, None] == request_ids[None, :]).astype(jnp.int32), 0)
    last_fill = jax.random.randint(subkeys[4], (REQUESTS,), 1, PAGE + 1)
    lengths = jnp.where(counts > 0, (counts - 1) * PAGE + last_fill, 0)
    lengths = jnp.where(request_ids == chosen, LEN_PAGES * PAGE, lengths)
    placing = jax.random.permutation(subkeys[5], POOL)
    slot_owner = jnp.zeros((POOL,), jnp.int32).at[placing].set(owners.astype(jnp.int32))
    slot_page = jnp.zeros((POOL,), jnp.int32).at[placing].set(page_rank.astype(jnp.int32))
    return (slot_owner, slot_page, lengths.astype(jnp.int32))


def draw_raw_q(key, part):
    return rising_features(key, 31)


def draw_raw_k(key, part):
    return rising_features(key, 37)


def draw_raw_v(key, part):
    noise_key = jax.random.fold_in(key, 43)
    return jnp.clip(jax.random.normal(noise_key, (ROWS, HEADS * HD), jnp.float32), -6.0, 6.0).astype(jnp.bfloat16)


def draw_prefix_keys(key, part):
    return cache_keys(key, 71, (GROUPS, PRE_PAGES))


def draw_prefix_values(key, part):
    return cache_values(key, 71, (GROUPS, PRE_PAGES))


def draw_key_cache(key, part):
    return cache_keys(key, 73, (POOL,))


def draw_value_cache(key, part):
    return cache_values(key, 73, (POOL,))


def draw_slot_owner(key, part):
    return allocate(jax.random.fold_in(key, 17))[0]


def draw_slot_page(key, part):
    return allocate(jax.random.fold_in(key, 17))[1]


def draw_cache_lengths(key, part):
    return allocate(jax.random.fold_in(key, 17))[2]


def draw_span_offsets(key, part):
    subkeys = jax.random.split(jax.random.fold_in(key, 23), 2)
    offsets = jax.random.randint(subkeys[0], (GROUPS,), 0, PRE_PAGES * PAGE + 1)
    longest = jax.random.randint(subkeys[1], (), 0, GROUPS)
    return offsets.at[longest].set(PRE_PAGES * PAGE).astype(jnp.int32)


def steps_of(key, extent, cuts, low, top_value):
    level, own = 1.0, jax.random.fold_in(key, 6)
    for axis_at, parts in cuts:
        steps = jnp.exp(jax.random.uniform(jax.random.fold_in(own, axis_at), (parts,), jnp.float32, low / len(cuts), top_value / len(cuts)))
        level = level * jnp.repeat(steps, extent[axis_at] // parts).reshape([-1 if axis == axis_at else 1 for axis in range(len(extent))])
    return level


def scatter_about(rng, shape, scale, most, pieces=(), kind=jnp.bfloat16):
    gain = steps_of(rng, shape, pieces, -0.22, 0.18) if pieces else 1.0
    entries = jax.random.normal(rng, shape, jnp.float32) * scale * gain
    return jnp.minimum(jnp.maximum(entries, -most), most).astype(kind)


def setup_inputs(seed: int = 0) -> dict:
    arg_keys = jax.random.split(jax.random.key(seed), 17)
    hidden = scatter_about(arg_keys[0], (ROWS, D), 1.0, 6.0, ((0, 32), (1, 8)))
    raw_q = draw_raw_q(jax.random.fold_in(arg_keys[16], 71), 0)
    raw_k = draw_raw_k(jax.random.fold_in(arg_keys[16], 71), 0)
    raw_v = draw_raw_v(jax.random.fold_in(arg_keys[16], 71), 0)
    q_gain = jnp.clip(jnp.exp(math.log(2.0) - 1.3862944 * jax.random.uniform(arg_keys[4], (HEADS * HD,), jnp.float32) ** steps_of(arg_keys[4], (HEADS * HD,), ((0, 8),), -0.2, 0.2)), 0.5, 2.0)
    k_gain = jnp.clip(jnp.exp(math.log(2.0) - 1.3862944 * jax.random.uniform(arg_keys[5], (HEADS * HD,), jnp.float32) ** steps_of(arg_keys[5], (HEADS * HD,), ((0, 8),), -0.2, 0.2)), 0.5, 2.0)
    out_weight = scatter_about(arg_keys[6], (HEADS * HD, D), (HEADS * HD) ** -0.5, 0.109375, ((0, 8),))
    post_gain = jnp.clip(1.0 + 0.15 * jax.random.normal(arg_keys[7], (D,), jnp.float32), 0.25, 1.75)
    prefix_keys = draw_prefix_keys(jax.random.fold_in(arg_keys[16], 71), 0)
    prefix_values = draw_prefix_values(jax.random.fold_in(arg_keys[16], 71), 0)
    key_cache = draw_key_cache(jax.random.fold_in(arg_keys[16], 71), 0)
    value_cache = draw_value_cache(jax.random.fold_in(arg_keys[16], 71), 0)
    slot_owner = draw_slot_owner(jax.random.fold_in(arg_keys[16], 71), 0)
    slot_page = draw_slot_page(jax.random.fold_in(arg_keys[16], 71), 0)
    cache_lengths = draw_cache_lengths(jax.random.fold_in(arg_keys[16], 71), 0)
    span_offsets = draw_span_offsets(jax.random.fold_in(arg_keys[16], 71), 0)
    return dict(hidden=hidden, raw_q=raw_q, raw_k=raw_k, raw_v=raw_v, q_gain=q_gain, k_gain=k_gain, out_weight=out_weight, post_gain=post_gain, prefix_keys=prefix_keys, prefix_values=prefix_values, key_cache=key_cache, value_cache=value_cache, slot_owner=slot_owner, slot_page=slot_page, cache_lengths=cache_lengths, span_offsets=span_offsets)


EPSILON = 1e-06
THETA = 500000.0
NEGATIVE = -1e+30

def rotate(values, positions):
    half_width = values.shape[-1] // 2
    frequency = THETA ** (-(jnp.arange(half_width, dtype=jnp.float32) * 2.0 / values.shape[-1]))
    angles = positions.astype(jnp.float32)[:, None] * frequency[None, :]
    cosine = jnp.cos(angles)[:, None, :]
    sine_part = jnp.sin(angles)[:, None, :]
    first_half = values[..., :half_width]
    second = values[..., half_width:]
    return jnp.concatenate([first_half * cosine - second * sine_part, second * cosine + first_half * sine_part], -1)

def rounded(values):
    return lax.optimization_barrier(values.astype(jnp.bfloat16)).astype(jnp.float32)

def reference(hidden, raw_q, raw_k, raw_v, q_gain, k_gain, out_weight, post_gain, prefix_keys, prefix_values, key_cache, value_cache, slot_owner, slot_page, cache_lengths, span_offsets):
    rows_group = SPAN + DEC
    score_scale = HD ** (-0.5)
    positions = jnp.concatenate([span_offsets[:, None] + jnp.arange(SPAN, dtype=jnp.int32)[None, :], cache_lengths.reshape(GROUPS, DEC)], 1).reshape(-1)
    float_query = raw_q.astype(jnp.float32)
    float_key = raw_k.astype(jnp.float32)
    normed_query = float_query * lax.rsqrt(lax.optimization_barrier(jnp.mean(float_query * float_query, 1, keepdims=True)) + EPSILON) * q_gain[None, :]
    normed_key = float_key * lax.rsqrt(lax.optimization_barrier(jnp.mean(float_key * float_key, 1, keepdims=True)) + EPSILON) * k_gain[None, :]
    query = rotate(normed_query.reshape(-1, HEADS, HD), positions).astype(jnp.bfloat16)
    key_rows = rotate(normed_key.reshape(-1, HEADS, HD), positions).astype(jnp.bfloat16)
    value_rows = raw_v.reshape(-1, HEADS, HD)
    query_grid = query.reshape(GROUPS, rows_group, HEADS, HD)
    key_grid = key_rows.reshape(GROUPS, rows_group, HEADS, HD)
    value_grid = value_rows.reshape(GROUPS, rows_group, HEADS, HD)
    causal = jnp.arange(SPAN, dtype=jnp.int32)[:, None] >= jnp.arange(SPAN, dtype=jnp.int32)[None, :]
    prefix_length = PRE_PAGES * PAGE

    def span_group(index):
        span_query = query_grid[index, :SPAN].astype(jnp.float32)
        all_keys = jnp.concatenate([prefix_keys[index].reshape(prefix_length, HEADS, HD), key_grid[index, :SPAN]], 0).astype(jnp.float32)
        all_values = jnp.concatenate([prefix_values[index].reshape(prefix_length, HEADS, HD), value_grid[index, :SPAN]], 0).astype(jnp.float32)
        prefix_mask = jnp.arange(prefix_length, dtype=jnp.int32) < span_offsets[index]
        key_mask = jnp.concatenate([jnp.broadcast_to(prefix_mask[None, :], (SPAN, prefix_length)), causal], 1)
        scores = jnp.einsum('qhd,khd->qhk', span_query, all_keys) * score_scale
        masked = jnp.where(key_mask[:, None, :], scores, NEGATIVE)
        top_score = lax.optimization_barrier(jnp.max(masked, -1, keepdims=True))
        exp_terms = jnp.where(key_mask[:, None, :], jnp.exp(masked - top_score), 0.0)
        numerator = jnp.einsum('qhk,khd->qhd', rounded(exp_terms), all_values)
        return numerator / lax.optimization_barrier(jnp.sum(exp_terms, -1))[..., None]
    span_out = lax.map(span_group, jnp.arange(GROUPS, dtype=jnp.int32))
    pool_keys = key_cache.astype(jnp.float32).reshape(-1, HEADS, HD)
    pool_values = value_cache.astype(jnp.float32).reshape(-1, HEADS, HD)
    pool_pos = (slot_page[:, None] * PAGE + jnp.arange(PAGE, dtype=jnp.int32)[None, :]).reshape(-1)
    pool_owner = jnp.repeat(slot_owner, PAGE)

    def decode_request(index):
        row_index = index // DEC * rows_group + SPAN + index % DEC
        one_query = query[row_index].astype(jnp.float32)
        own_key = key_rows[row_index].astype(jnp.float32)
        own_value = value_rows[row_index].astype(jnp.float32)
        pool_scores = jnp.einsum('hd,khd->hk', one_query, pool_keys) * score_scale
        own_score = lax.optimization_barrier(jnp.sum(one_query * own_key, -1)) * score_scale
        key_mask = (pool_owner == index) & (pool_pos < cache_lengths[index])
        masked = jnp.where(key_mask[None, :], pool_scores, NEGATIVE)
        top_score = jnp.maximum(lax.optimization_barrier(jnp.max(masked, -1)), own_score)
        pool_terms = jnp.where(key_mask[None, :], jnp.exp(masked - top_score[:, None]), 0.0)
        own_term = jnp.exp(own_score - top_score)
        weight_sum = lax.optimization_barrier(jnp.sum(pool_terms, -1)) + own_term
        numerator = jnp.einsum('hk,khd->hd', rounded(pool_terms), pool_values) + rounded(own_term)[:, None] * own_value
        return numerator / weight_sum[:, None]
    decode_out = lax.map(decode_request, jnp.arange(REQUESTS, dtype=jnp.int32))
    merged = jnp.concatenate([span_out, decode_out.reshape(GROUPS, DEC, HEADS, HD)], 1)
    attention = merged.reshape(GROUPS * rows_group, HEADS * HD).astype(jnp.bfloat16)
    projected = jnp.dot(attention, out_weight, preferred_element_type=jnp.float32)
    normed = projected * lax.rsqrt(lax.optimization_barrier(jnp.mean(projected * projected, 1, keepdims=True)) + EPSILON) * post_gain[None, :]
    return (hidden.astype(jnp.float32) + normed).astype(jnp.bfloat16)
```

```python
import jax
import jax.numpy as jnp
from jax import lax
from jax.sharding import PartitionSpec as P

HD = 128
SPAN = 288
DEC = 8


EPSILON = 1e-06
THETA = 500000.0
NEGATIVE = -1e30


def rotate(values, positions):
    half_width = values.shape[-1] // 2
    frequency = THETA ** (-(jnp.arange(half_width, dtype=jnp.float32) * 2.0 / values.shape[-1]))
    angles = positions.astype(jnp.float32)[:, None] * frequency[None, :]
    cosine = jnp.cos(angles)[:, None, :]
    sine_part = jnp.sin(angles)[:, None, :]
    first_half = values[..., :half_width]
    second = values[..., half_width:]
    return jnp.concatenate(
        [first_half * cosine - second * sine_part, second * cosine + first_half * sine_part], -1
    )


def softmax_part(scores, key_mask, values, form):
    masked = jnp.where(key_mask, scores, NEGATIVE)
    top_score = jnp.max(masked, -1)
    exp_terms = jnp.where(key_mask, jnp.exp(masked - top_score[..., None]), 0.0)
    weight_sum = jnp.sum(exp_terms, -1)
    numerator = jnp.einsum(
        form, exp_terms.astype(jnp.bfloat16), values, preferred_element_type=jnp.float32
    )
    return (top_score, weight_sum, numerator)


def merge_parts(top_scores, weight_sums, numerators):
    best_score = jnp.max(top_scores, 0)
    factor = jnp.exp(top_scores - best_score[None])
    weight_sum = jnp.sum(factor * weight_sums, 0)
    numerator = jnp.sum(factor[..., None] * numerators, 0)
    return numerator / weight_sum[..., None]


def body(
    hidden,
    raw_q,
    raw_k,
    raw_v,
    q_gain,
    k_gain,
    out_weight,
    post_gain,
    prefix_keys,
    prefix_values,
    key_cache,
    value_cache,
    slot_owner,
    slot_page,
    cache_lengths,
    span_offsets,
):
    groups = lax.axis_size("req")
    my_group = lax.axis_index("req")
    tp_count = lax.axis_size("tp")
    rows_group = SPAN + DEC
    local_width = raw_q.shape[1]
    local_heads = local_width // HD
    requests = groups * DEC
    score_scale = HD ** (-0.5)
    page_rows = key_cache.shape[1]

    own_keys = lax.all_to_all(prefix_keys, "req", split_axis=0, concat_axis=1, tiled=True)
    own_values = lax.all_to_all(prefix_values, "req", split_axis=0, concat_axis=1, tiled=True)
    prefix_len = own_keys.shape[1] * page_rows
    own_keys = own_keys.reshape(prefix_len, local_heads, HD)
    own_values = own_values.reshape(prefix_len, local_heads, HD)

    own_lengths = lax.dynamic_slice_in_dim(cache_lengths, my_group * DEC, DEC)
    positions = jnp.concatenate(
        [span_offsets[my_group] + jnp.arange(SPAN, dtype=jnp.int32), own_lengths]
    )
    float_query = raw_q.astype(jnp.float32)
    float_key = raw_k.astype(jnp.float32)
    query_power, key_power = lax.psum(
        (jnp.sum(float_query * float_query, 1), jnp.sum(float_key * float_key, 1)), "tp"
    )
    full_width = local_width * tp_count
    normed_query = (
        float_query * lax.rsqrt(query_power / full_width + EPSILON)[:, None] * q_gain[None, :]
    )
    normed_key = float_key * lax.rsqrt(key_power / full_width + EPSILON)[:, None] * k_gain[None, :]
    query = rotate(normed_query.reshape(rows_group, local_heads, HD), positions).astype(
        jnp.bfloat16
    )
    key_rows = rotate(normed_key.reshape(rows_group, local_heads, HD), positions).astype(
        jnp.bfloat16
    )
    value_rows = raw_v.reshape(rows_group, local_heads, HD)

    decode_queries = lax.all_gather(query[SPAN:], "req", axis=0, tiled=True)
    live_slot = slot_owner >= 0
    owner_index = jnp.maximum(slot_owner, 0)
    slot_queries = decode_queries[owner_index]
    slot_keys = key_cache.reshape(key_cache.shape[0], page_rows, local_heads, HD)
    slot_values = value_cache.reshape(value_cache.shape[0], page_rows, local_heads, HD)
    scores = (
        jnp.einsum("shd,sphd->shp", slot_queries, slot_keys, preferred_element_type=jnp.float32)
        * score_scale
    )
    key_pos = slot_page[:, None] * page_rows + jnp.arange(page_rows, dtype=jnp.int32)[None, :]
    key_mask = live_slot[:, None] & (key_pos < cache_lengths[owner_index][:, None])
    top_score, weight_sum, numerator = softmax_part(
        scores, key_mask[:, None, :], slot_values, "shp,sphd->shd"
    )
    member = slot_owner[None, :] == jnp.arange(requests, dtype=jnp.int32)[:, None]
    best_score = jnp.max(jnp.where(member[:, :, None], top_score[None], NEGATIVE), 1)
    factor = jnp.where(member[:, :, None], jnp.exp(top_score[None] - best_score[:, None]), 0.0)
    request_total = jnp.einsum("rsh,sh->rh", factor, weight_sum, precision=lax.Precision.HIGHEST)
    request_numerator = jnp.einsum(
        "rsh,shd->rhd", factor, numerator, precision=lax.Precision.HIGHEST
    )
    packed = jnp.concatenate(
        [request_numerator, best_score[..., None], request_total[..., None]], -1
    )
    back = lax.all_to_all(packed, "req", split_axis=0, concat_axis=0, tiled=True)
    back = back.reshape(groups, DEC, local_heads, HD + 2)
    own_scores = (
        jnp.sum(query[SPAN:].astype(jnp.float32) * key_rows[SPAN:].astype(jnp.float32), -1)
        * score_scale
    )
    decode_out = merge_parts(
        jnp.concatenate([back[..., HD], own_scores[None]], 0),
        jnp.concatenate([back[..., HD + 1], jnp.ones_like(own_scores)[None]], 0),
        jnp.concatenate([back[..., :HD], value_rows[SPAN:].astype(jnp.float32)[None]], 0),
    )

    span_query = query[:SPAN]
    causal = jnp.arange(SPAN)[:, None] >= jnp.arange(SPAN)[None, :]
    prefix_mask = jnp.arange(prefix_len, dtype=jnp.int32) < span_offsets[my_group]
    pre_scores = (
        jnp.einsum("qhd,khd->qhk", span_query, own_keys, preferred_element_type=jnp.float32)
        * score_scale
    )
    self_scores = (
        jnp.einsum("qhd,khd->qhk", span_query, key_rows[:SPAN], preferred_element_type=jnp.float32)
        * score_scale
    )
    pre_masked = jnp.where(prefix_mask[None, None, :], pre_scores, NEGATIVE)
    self_masked = jnp.where(causal[:, None, :], self_scores, NEGATIVE)
    top = jnp.maximum(jnp.max(pre_masked, -1), jnp.max(self_masked, -1))
    pre_exp = jnp.where(prefix_mask[None, None, :], jnp.exp(pre_masked - top[..., None]), 0.0)
    self_exp = jnp.where(causal[:, None, :], jnp.exp(self_masked - top[..., None]), 0.0)
    total = jnp.sum(pre_exp, -1) + jnp.sum(self_exp, -1)
    span_numerator = jnp.einsum(
        "qhk,khd->qhd", pre_exp.astype(jnp.bfloat16), own_values, preferred_element_type=jnp.float32
    ) + jnp.einsum(
        "qhk,khd->qhd",
        self_exp.astype(jnp.bfloat16),
        value_rows[:SPAN],
        preferred_element_type=jnp.float32,
    )
    span_out = span_numerator / total[..., None]

    merged = jnp.concatenate([span_out, decode_out], 0)
    attention = merged.reshape(rows_group, local_width).astype(jnp.bfloat16)
    share_width = post_gain.shape[0]
    partial = jnp.dot(attention, out_weight, preferred_element_type=jnp.float32)
    my_share = lax.psum_scatter(partial, "tp", scatter_dimension=1, tiled=True)
    power = lax.psum(jnp.sum(my_share * my_share, 1), "tp")
    inverse = lax.rsqrt(power / (share_width * tp_count) + EPSILON)
    normed = my_share * inverse[:, None]
    return (hidden.astype(jnp.float32) + normed * post_gain[None, :]).astype(jnp.bfloat16)


def solution(mesh):
    return jax.shard_map(
        body,
        mesh=mesh,
        in_specs=(
            P("req", "tp"),
            P("req", "tp"),
            P("req", "tp"),
            P("req", "tp"),
            P("tp"),
            P("tp"),
            P("tp", None),
            P("tp"),
            P(None, "req", None, "tp"),
            P(None, "req", None, "tp"),
            P("req", None, "tp"),
            P("req", None, "tp"),
            P("req"),
            P("req"),
            P(),
            P(),
        ),
        out_specs=P("req", "tp"),
        check_vma=False,
    )
```

```python
import jax
import jax.numpy as jnp
from jax import lax
from jax.sharding import PartitionSpec as P

HD = 128
SPAN = 288
DEC = 8


EPSILON = 1e-06
THETA = 500000.0
NEGATIVE = -1e30


def rotate(values, positions):
    half_width = values.shape[-1] // 2
    frequency = THETA ** (-(jnp.arange(half_width, dtype=jnp.float32) * 2.0 / values.shape[-1]))
    angles = positions.astype(jnp.float32)[:, None] * frequency[None, :]
    cosine = jnp.cos(angles)[:, None, :]
    sine_part = jnp.sin(angles)[:, None, :]
    first_half = values[..., :half_width]
    second = values[..., half_width:]
    return jnp.concatenate(
        [first_half * cosine - second * sine_part, second * cosine + first_half * sine_part], -1
    )


def softmax_part(scores, key_mask, values, form):
    masked = jnp.where(key_mask, scores, NEGATIVE)
    top_score = jnp.max(masked, -1)
    exp_terms = jnp.where(key_mask, jnp.exp(masked - top_score[..., None]), 0.0)
    weight_sum = jnp.sum(exp_terms, -1)
    numerator = jnp.einsum(
        form, exp_terms.astype(jnp.bfloat16), values, preferred_element_type=jnp.float32
    )
    return (top_score, weight_sum, numerator)


def merge_parts(top_scores, weight_sums, numerators):
    best_score = jnp.max(top_scores, 0)
    factor = jnp.exp(top_scores - best_score[None])
    weight_sum = jnp.sum(factor * weight_sums, 0)
    numerator = jnp.sum(factor[..., None] * numerators, 0)
    return numerator / weight_sum[..., None]


def body(
    hidden,
    raw_q,
    raw_k,
    raw_v,
    q_gain,
    k_gain,
    out_weight,
    post_gain,
    prefix_keys,
    prefix_values,
    key_cache,
    value_cache,
    slot_owner,
    slot_page,
    cache_lengths,
    span_offsets,
):
    groups = lax.axis_size("req")
    my_group = lax.axis_index("req")
    tp_count = lax.axis_size("tp")
    rows_group = SPAN + DEC
    local_width = raw_q.shape[1]
    local_heads = local_width // HD
    requests = groups * DEC
    score_scale = HD ** (-0.5)
    page_rows = key_cache.shape[1]

    pages_here = prefix_keys.shape[1]
    both = jnp.concatenate([prefix_keys, prefix_values], 1)
    both = lax.all_to_all(both, "req", split_axis=0, concat_axis=1, tiled=True)
    both = both.reshape(groups, 2, pages_here, page_rows, local_heads, HD)
    prefix_len = groups * pages_here * page_rows
    own_keys = both[:, 0].reshape(prefix_len, local_heads, HD)
    own_values = both[:, 1].reshape(prefix_len, local_heads, HD)

    own_lengths = lax.dynamic_slice_in_dim(cache_lengths, my_group * DEC, DEC)
    positions = jnp.concatenate(
        [span_offsets[my_group] + jnp.arange(SPAN, dtype=jnp.int32), own_lengths]
    )
    float_query = raw_q.astype(jnp.float32)
    float_key = raw_k.astype(jnp.float32)
    query_power, key_power = lax.psum(
        (jnp.sum(float_query * float_query, 1), jnp.sum(float_key * float_key, 1)), "tp"
    )
    full_width = local_width * tp_count
    normed_query = (
        float_query * lax.rsqrt(query_power / full_width + EPSILON)[:, None] * q_gain[None, :]
    )
    normed_key = float_key * lax.rsqrt(key_power / full_width + EPSILON)[:, None] * k_gain[None, :]
    query = rotate(normed_query.reshape(rows_group, local_heads, HD), positions).astype(
        jnp.bfloat16
    )
    key_rows = rotate(normed_key.reshape(rows_group, local_heads, HD), positions).astype(
        jnp.bfloat16
    )
    value_rows = raw_v.reshape(rows_group, local_heads, HD)

    placed = lax.dynamic_update_slice_in_dim(
        jnp.zeros((requests, local_heads, HD), jnp.bfloat16), query[SPAN:], my_group * DEC, 0
    )
    decode_queries = lax.psum(placed, "req")
    live_slot = slot_owner >= 0
    owner_index = jnp.maximum(slot_owner, 0)
    slot_queries = decode_queries[owner_index]
    slot_keys = key_cache.reshape(key_cache.shape[0], page_rows, local_heads, HD)
    slot_values = value_cache.reshape(value_cache.shape[0], page_rows, local_heads, HD)
    scores = (
        jnp.einsum("shd,sphd->shp", slot_queries, slot_keys, preferred_element_type=jnp.float32)
        * score_scale
    )
    key_pos = slot_page[:, None] * page_rows + jnp.arange(page_rows, dtype=jnp.int32)[None, :]
    key_mask = live_slot[:, None] & (key_pos < cache_lengths[owner_index][:, None])
    top_score, weight_sum, numerator = softmax_part(
        scores, key_mask[:, None, :], slot_values, "shp,sphd->shd"
    )
    member = slot_owner[None, :] == jnp.arange(requests, dtype=jnp.int32)[:, None]
    best_score = jnp.max(jnp.where(member[:, :, None], top_score[None], NEGATIVE), 1)
    factor = jnp.where(member[:, :, None], jnp.exp(top_score[None] - best_score[:, None]), 0.0)
    request_total = jnp.einsum("rsh,sh->rh", factor, weight_sum, precision=lax.Precision.HIGHEST)
    request_numerator = jnp.einsum(
        "rsh,shd->rhd", factor, numerator, precision=lax.Precision.HIGHEST
    )
    packed = jnp.concatenate(
        [request_numerator, best_score[..., None], request_total[..., None]], -1
    )
    back = lax.all_to_all(packed, "req", split_axis=0, concat_axis=0, tiled=True)
    back = back.reshape(groups, DEC, local_heads, HD + 2)
    own_scores = (
        jnp.sum(query[SPAN:].astype(jnp.float32) * key_rows[SPAN:].astype(jnp.float32), -1)
        * score_scale
    )
    decode_out = merge_parts(
        jnp.concatenate([back[..., HD], own_scores[None]], 0),
        jnp.concatenate([back[..., HD + 1], jnp.ones_like(own_scores)[None]], 0),
        jnp.concatenate([back[..., :HD], value_rows[SPAN:].astype(jnp.float32)[None]], 0),
    )

    span_query = query[:SPAN]
    causal = jnp.arange(SPAN)[:, None] >= jnp.arange(SPAN)[None, :]
    prefix_mask = jnp.arange(prefix_len, dtype=jnp.int32) < span_offsets[my_group]
    pre_scores = (
        jnp.einsum("qhd,khd->qhk", span_query, own_keys, preferred_element_type=jnp.float32)
        * score_scale
    )
    self_scores = (
        jnp.einsum("qhd,khd->qhk", span_query, key_rows[:SPAN], preferred_element_type=jnp.float32)
        * score_scale
    )
    pre_masked = jnp.where(prefix_mask[None, None, :], pre_scores, NEGATIVE)
    self_masked = jnp.where(causal[:, None, :], self_scores, NEGATIVE)
    top = jnp.maximum(jnp.max(pre_masked, -1), jnp.max(self_masked, -1))
    pre_exp = jnp.where(prefix_mask[None, None, :], jnp.exp(pre_masked - top[..., None]), 0.0)
    self_exp = jnp.where(causal[:, None, :], jnp.exp(self_masked - top[..., None]), 0.0)
    total = jnp.sum(pre_exp, -1) + jnp.sum(self_exp, -1)
    span_numerator = jnp.einsum(
        "qhk,khd->qhd", pre_exp.astype(jnp.bfloat16), own_values, preferred_element_type=jnp.float32
    ) + jnp.einsum(
        "qhk,khd->qhd",
        self_exp.astype(jnp.bfloat16),
        value_rows[:SPAN],
        preferred_element_type=jnp.float32,
    )
    span_out = span_numerator / total[..., None]

    merged = jnp.concatenate([span_out, decode_out], 0)
    attention = merged.reshape(rows_group, local_width).astype(jnp.bfloat16)
    share_width = post_gain.shape[0]
    partial = jnp.dot(attention, out_weight, preferred_element_type=jnp.float32)
    my_share = lax.psum_scatter(partial, "tp", scatter_dimension=1, tiled=True)
    power = lax.psum(jnp.sum(my_share * my_share, 1), "tp")
    inverse = lax.rsqrt(power / (share_width * tp_count) + EPSILON)
    normed = my_share * inverse[:, None]
    return (hidden.astype(jnp.float32) + normed * post_gain[None, :]).astype(jnp.bfloat16)


def solution(mesh):
    return jax.shard_map(
        body,
        mesh=mesh,
        in_specs=(
            P("req", "tp"),
            P("req", "tp"),
            P("req", "tp"),
            P("req", "tp"),
            P("tp"),
            P("tp"),
            P("tp", None),
            P("tp"),
            P(None, "req", None, "tp"),
            P(None, "req", None, "tp"),
            P("req", None, "tp"),
            P("req", None, "tp"),
            P("req"),
            P("req"),
            P(),
            P(),
        ),
        out_specs=P("req", "tp"),
        check_vma=False,
    )
```

```python
import jax
import jax.numpy as jnp
from jax import lax
from jax.sharding import PartitionSpec as P

HD = 128
SPAN = 288
DEC = 8


EPSILON = 1e-06
THETA = 500000.0
NEGATIVE = -1e30


def rotate(values, positions):
    half_width = values.shape[-1] // 2
    frequency = THETA ** (-(jnp.arange(half_width, dtype=jnp.float32) * 2.0 / values.shape[-1]))
    angles = positions.astype(jnp.float32)[:, None] * frequency[None, :]
    cosine = jnp.cos(angles)[:, None, :]
    sine_part = jnp.sin(angles)[:, None, :]
    first_half = values[..., :half_width]
    second = values[..., half_width:]
    return jnp.concatenate(
        [first_half * cosine - second * sine_part, second * cosine + first_half * sine_part], -1
    )


def softmax_part(scores, key_mask, values, form):
    masked = jnp.where(key_mask, scores, NEGATIVE)
    top_score = jnp.max(masked, -1)
    exp_terms = jnp.where(key_mask, jnp.exp(masked - top_score[..., None]), 0.0)
    weight_sum = jnp.sum(exp_terms, -1)
    numerator = jnp.einsum(
        form, exp_terms.astype(jnp.bfloat16), values, preferred_element_type=jnp.float32
    )
    return (top_score, weight_sum, numerator)


def merge_parts(top_scores, weight_sums, numerators):
    best_score = jnp.max(top_scores, 0)
    factor = jnp.exp(top_scores - best_score[None])
    weight_sum = jnp.sum(factor * weight_sums, 0)
    numerator = jnp.sum(factor[..., None] * numerators, 0)
    return numerator / weight_sum[..., None]


def body(
    hidden,
    raw_q,
    raw_k,
    raw_v,
    q_gain,
    k_gain,
    out_weight,
    post_gain,
    prefix_keys,
    prefix_values,
    key_cache,
    value_cache,
    slot_owner,
    slot_page,
    cache_lengths,
    span_offsets,
):
    groups = lax.axis_size("req")
    my_group = lax.axis_index("req")
    tp_count = lax.axis_size("tp")
    rows_group = SPAN + DEC
    local_width = raw_q.shape[1]
    local_heads = local_width // HD
    requests = groups * DEC
    score_scale = HD ** (-0.5)
    page_rows = key_cache.shape[1]


    own_lengths = lax.dynamic_slice_in_dim(cache_lengths, my_group * DEC, DEC)
    positions = jnp.concatenate(
        [span_offsets[my_group] + jnp.arange(SPAN, dtype=jnp.int32), own_lengths]
    )
    float_query = raw_q.astype(jnp.float32)
    float_key = raw_k.astype(jnp.float32)
    query_power, key_power = lax.psum(
        (jnp.sum(float_query * float_query, 1), jnp.sum(float_key * float_key, 1)), "tp"
    )
    full_width = local_width * tp_count
    normed_query = (
        float_query * lax.rsqrt(query_power / full_width + EPSILON)[:, None] * q_gain[None, :]
    )
    normed_key = float_key * lax.rsqrt(key_power / full_width + EPSILON)[:, None] * k_gain[None, :]
    query = rotate(normed_query.reshape(rows_group, local_heads, HD), positions).astype(
        jnp.bfloat16
    )
    key_rows = rotate(normed_key.reshape(rows_group, local_heads, HD), positions).astype(
        jnp.bfloat16
    )
    value_rows = raw_v.reshape(rows_group, local_heads, HD)

    pages_here = prefix_keys.shape[1]
    block_rows = pages_here * page_rows
    outgoing = jnp.concatenate(
        [
            prefix_keys.reshape(groups, block_rows, local_width),
            prefix_values.reshape(groups, block_rows, local_width),
            jnp.broadcast_to(
                query[None, SPAN:].reshape(1, DEC, local_width), (groups, DEC, local_width)
            ),
        ],
        1,
    )
    incoming = lax.all_to_all(outgoing, "req", split_axis=0, concat_axis=0, tiled=True)
    prefix_len = groups * block_rows
    own_keys = incoming[:, :block_rows].reshape(prefix_len, local_heads, HD)
    own_values = incoming[:, block_rows : 2 * block_rows].reshape(prefix_len, local_heads, HD)
    decode_queries = incoming[:, 2 * block_rows :].reshape(requests, local_heads, HD)
    live_slot = slot_owner >= 0
    owner_index = jnp.maximum(slot_owner, 0)
    slot_queries = decode_queries[owner_index]
    slot_keys = key_cache.reshape(key_cache.shape[0], page_rows, local_heads, HD)
    slot_values = value_cache.reshape(value_cache.shape[0], page_rows, local_heads, HD)
    scores = (
        jnp.einsum("shd,sphd->shp", slot_queries, slot_keys, preferred_element_type=jnp.float32)
        * score_scale
    )
    key_pos = slot_page[:, None] * page_rows + jnp.arange(page_rows, dtype=jnp.int32)[None, :]
    key_mask = live_slot[:, None] & (key_pos < cache_lengths[owner_index][:, None])
    top_score, weight_sum, numerator = softmax_part(
        scores, key_mask[:, None, :], slot_values, "shp,sphd->shd"
    )
    member = slot_owner[None, :] == jnp.arange(requests, dtype=jnp.int32)[:, None]
    best_score = jnp.max(jnp.where(member[:, :, None], top_score[None], NEGATIVE), 1)
    factor = jnp.where(member[:, :, None], jnp.exp(top_score[None] - best_score[:, None]), 0.0)
    request_total = jnp.einsum("rsh,sh->rh", factor, weight_sum, precision=lax.Precision.HIGHEST)
    request_numerator = jnp.einsum(
        "rsh,shd->rhd", factor, numerator, precision=lax.Precision.HIGHEST
    )
    packed = jnp.concatenate(
        [request_numerator, best_score[..., None], request_total[..., None]], -1
    )
    back = lax.all_to_all(packed, "req", split_axis=0, concat_axis=0, tiled=True)
    back = back.reshape(groups, DEC, local_heads, HD + 2)
    own_scores = (
        jnp.sum(query[SPAN:].astype(jnp.float32) * key_rows[SPAN:].astype(jnp.float32), -1)
        * score_scale
    )
    decode_out = merge_parts(
        jnp.concatenate([back[..., HD], own_scores[None]], 0),
        jnp.concatenate([back[..., HD + 1], jnp.ones_like(own_scores)[None]], 0),
        jnp.concatenate([back[..., :HD], value_rows[SPAN:].astype(jnp.float32)[None]], 0),
    )

    span_query = query[:SPAN]
    causal = jnp.arange(SPAN)[:, None] >= jnp.arange(SPAN)[None, :]
    prefix_mask = jnp.arange(prefix_len, dtype=jnp.int32) < span_offsets[my_group]
    pre_scores = (
        jnp.einsum("qhd,khd->qhk", span_query, own_keys, preferred_element_type=jnp.float32)
        * score_scale
    )
    self_scores = (
        jnp.einsum("qhd,khd->qhk", span_query, key_rows[:SPAN], preferred_element_type=jnp.float32)
        * score_scale
    )
    pre_masked = jnp.where(prefix_mask[None, None, :], pre_scores, NEGATIVE)
    self_masked = jnp.where(causal[:, None, :], self_scores, NEGATIVE)
    top = jnp.maximum(jnp.max(pre_masked, -1), jnp.max(self_masked, -1))
    pre_exp = jnp.where(prefix_mask[None, None, :], jnp.exp(pre_masked - top[..., None]), 0.0)
    self_exp = jnp.where(causal[:, None, :], jnp.exp(self_masked - top[..., None]), 0.0)
    total = jnp.sum(pre_exp, -1) + jnp.sum(self_exp, -1)
    span_numerator = jnp.einsum(
        "qhk,khd->qhd", pre_exp.astype(jnp.bfloat16), own_values, preferred_element_type=jnp.float32
    ) + jnp.einsum(
        "qhk,khd->qhd",
        self_exp.astype(jnp.bfloat16),
        value_rows[:SPAN],
        preferred_element_type=jnp.float32,
    )
    span_out = span_numerator / total[..., None]

    merged = jnp.concatenate([span_out, decode_out], 0)
    attention = merged.reshape(rows_group, local_width).astype(jnp.bfloat16)
    share_width = post_gain.shape[0]
    partial = jnp.dot(attention, out_weight, preferred_element_type=jnp.float32)
    my_share = lax.psum_scatter(partial, "tp", scatter_dimension=1, tiled=True)
    power = lax.psum(jnp.sum(my_share * my_share, 1), "tp")
    inverse = lax.rsqrt(power / (share_width * tp_count) + EPSILON)
    normed = my_share * inverse[:, None]
    return (hidden.astype(jnp.float32) + normed * post_gain[None, :]).astype(jnp.bfloat16)


def solution(mesh):
    return jax.shard_map(
        body,
        mesh=mesh,
        in_specs=(
            P("req", "tp"),
            P("req", "tp"),
            P("req", "tp"),
            P("req", "tp"),
            P("tp"),
            P("tp"),
            P("tp", None),
            P("tp"),
            P(None, "req", None, "tp"),
            P(None, "req", None, "tp"),
            P("req", None, "tp"),
            P("req", None, "tp"),
            P("req"),
            P("req"),
            P(),
            P(),
        ),
        out_specs=P("req", "tp"),
        check_vma=False,
    )
```

```python
import jax
import jax.numpy as jnp
from jax import lax
from jax.sharding import PartitionSpec as P

HD = 128
SPAN = 288
DEC = 8


EPSILON = 1e-06
THETA = 500000.0
NEGATIVE = -1e30


def rotate(values, positions):
    half_width = values.shape[-1] // 2
    frequency = THETA ** (-(jnp.arange(half_width, dtype=jnp.float32) * 2.0 / values.shape[-1]))
    angles = positions.astype(jnp.float32)[:, None] * frequency[None, :]
    cosine = jnp.cos(angles)[:, None, :]
    sine_part = jnp.sin(angles)[:, None, :]
    first_half = values[..., :half_width]
    second = values[..., half_width:]
    return jnp.concatenate(
        [first_half * cosine - second * sine_part, second * cosine + first_half * sine_part], -1
    )


def softmax_part(scores, key_mask, values, form):
    masked = jnp.where(key_mask, scores, NEGATIVE)
    top_score = jnp.max(masked, -1)
    exp_terms = jnp.where(key_mask, jnp.exp(masked - top_score[..., None]), 0.0)
    weight_sum = jnp.sum(exp_terms, -1)
    numerator = jnp.einsum(
        form, exp_terms.astype(jnp.bfloat16), values, preferred_element_type=jnp.float32
    )
    return (top_score, weight_sum, numerator)


def merge_parts(top_scores, weight_sums, numerators):
    best_score = jnp.max(top_scores, 0)
    factor = jnp.exp(top_scores - best_score[None])
    weight_sum = jnp.sum(factor * weight_sums, 0)
    numerator = jnp.sum(factor[..., None] * numerators, 0)
    return numerator / weight_sum[..., None]


def body(
    hidden,
    raw_q,
    raw_k,
    raw_v,
    q_gain,
    k_gain,
    out_weight,
    post_gain,
    prefix_keys,
    prefix_values,
    key_cache,
    value_cache,
    slot_owner,
    slot_page,
    cache_lengths,
    span_offsets,
):
    groups = lax.axis_size("req")
    my_group = lax.axis_index("req")
    tp_count = lax.axis_size("tp")
    rows_group = SPAN + DEC
    local_width = raw_q.shape[1]
    local_heads = local_width // HD
    requests = groups * DEC
    score_scale = HD ** (-0.5)
    page_rows = key_cache.shape[1]


    own_lengths = lax.dynamic_slice_in_dim(cache_lengths, my_group * DEC, DEC)
    positions = jnp.concatenate(
        [span_offsets[my_group] + jnp.arange(SPAN, dtype=jnp.int32), own_lengths]
    )
    float_query = raw_q.astype(jnp.float32)
    float_key = raw_k.astype(jnp.float32)
    query_power, key_power = lax.psum(
        (jnp.sum(float_query * float_query, 1), jnp.sum(float_key * float_key, 1)), "tp"
    )
    full_width = local_width * tp_count
    normed_query = (
        float_query * lax.rsqrt(query_power / full_width + EPSILON)[:, None] * q_gain[None, :]
    )
    normed_key = float_key * lax.rsqrt(key_power / full_width + EPSILON)[:, None] * k_gain[None, :]
    query = rotate(normed_query.reshape(rows_group, local_heads, HD), positions).astype(
        jnp.bfloat16
    )
    key_rows = rotate(normed_key.reshape(rows_group, local_heads, HD), positions).astype(
        jnp.bfloat16
    )
    value_rows = raw_v.reshape(rows_group, local_heads, HD)

    pages_here = prefix_keys.shape[1]
    block_rows = pages_here * page_rows
    outgoing = jnp.concatenate(
        [
            prefix_keys.reshape(groups, block_rows, local_width),
            jnp.broadcast_to(
                query[None, SPAN:].reshape(1, DEC, local_width), (groups, DEC, local_width)
            ),
        ],
        1,
    )
    incoming = lax.all_to_all(outgoing, "req", split_axis=0, concat_axis=0, tiled=True)
    own_values = lax.all_to_all(
        prefix_values.reshape(groups, block_rows, local_width),
        "req",
        split_axis=0,
        concat_axis=0,
        tiled=True,
    )
    prefix_len = groups * block_rows
    own_keys = incoming[:, :block_rows].reshape(prefix_len, local_heads, HD)
    own_values = own_values.reshape(prefix_len, local_heads, HD)
    decode_queries = incoming[:, block_rows:].reshape(requests, local_heads, HD)
    live_slot = slot_owner >= 0
    owner_index = jnp.maximum(slot_owner, 0)
    slot_queries = decode_queries[owner_index]
    slot_keys = key_cache.reshape(key_cache.shape[0], page_rows, local_heads, HD)
    slot_values = value_cache.reshape(value_cache.shape[0], page_rows, local_heads, HD)
    scores = (
        jnp.einsum("shd,sphd->shp", slot_queries, slot_keys, preferred_element_type=jnp.float32)
        * score_scale
    )
    key_pos = slot_page[:, None] * page_rows + jnp.arange(page_rows, dtype=jnp.int32)[None, :]
    key_mask = live_slot[:, None] & (key_pos < cache_lengths[owner_index][:, None])
    top_score, weight_sum, numerator = softmax_part(
        scores, key_mask[:, None, :], slot_values, "shp,sphd->shd"
    )
    member = slot_owner[None, :] == jnp.arange(requests, dtype=jnp.int32)[:, None]
    best_score = jnp.max(jnp.where(member[:, :, None], top_score[None], NEGATIVE), 1)
    factor = jnp.where(member[:, :, None], jnp.exp(top_score[None] - best_score[:, None]), 0.0)
    request_total = jnp.einsum("rsh,sh->rh", factor, weight_sum, precision=lax.Precision.HIGHEST)
    request_numerator = jnp.einsum(
        "rsh,shd->rhd", factor, numerator, precision=lax.Precision.HIGHEST
    )
    packed = jnp.concatenate(
        [request_numerator, best_score[..., None], request_total[..., None]], -1
    )
    back = lax.all_to_all(packed, "req", split_axis=0, concat_axis=0, tiled=True)
    back = back.reshape(groups, DEC, local_heads, HD + 2)
    own_scores = (
        jnp.sum(query[SPAN:].astype(jnp.float32) * key_rows[SPAN:].astype(jnp.float32), -1)
        * score_scale
    )
    decode_out = merge_parts(
        jnp.concatenate([back[..., HD], own_scores[None]], 0),
        jnp.concatenate([back[..., HD + 1], jnp.ones_like(own_scores)[None]], 0),
        jnp.concatenate([back[..., :HD], value_rows[SPAN:].astype(jnp.float32)[None]], 0),
    )

    span_query = query[:SPAN]
    causal = jnp.arange(SPAN)[:, None] >= jnp.arange(SPAN)[None, :]
    prefix_mask = jnp.arange(prefix_len, dtype=jnp.int32) < span_offsets[my_group]
    pre_scores = (
        jnp.einsum("qhd,khd->qhk", span_query, own_keys, preferred_element_type=jnp.float32)
        * score_scale
    )
    self_scores = (
        jnp.einsum("qhd,khd->qhk", span_query, key_rows[:SPAN], preferred_element_type=jnp.float32)
        * score_scale
    )
    pre_masked = jnp.where(prefix_mask[None, None, :], pre_scores, NEGATIVE)
    self_masked = jnp.where(causal[:, None, :], self_scores, NEGATIVE)
    top = jnp.maximum(jnp.max(pre_masked, -1), jnp.max(self_masked, -1))
    pre_exp = jnp.where(prefix_mask[None, None, :], jnp.exp(pre_masked - top[..., None]), 0.0)
    self_exp = jnp.where(causal[:, None, :], jnp.exp(self_masked - top[..., None]), 0.0)
    total = jnp.sum(pre_exp, -1) + jnp.sum(self_exp, -1)
    span_numerator = jnp.einsum(
        "qhk,khd->qhd", pre_exp.astype(jnp.bfloat16), own_values, preferred_element_type=jnp.float32
    ) + jnp.einsum(
        "qhk,khd->qhd",
        self_exp.astype(jnp.bfloat16),
        value_rows[:SPAN],
        preferred_element_type=jnp.float32,
    )
    span_out = span_numerator / total[..., None]

    merged = jnp.concatenate([span_out, decode_out], 0)
    attention = merged.reshape(rows_group, local_width).astype(jnp.bfloat16)
    share_width = post_gain.shape[0]
    partial = jnp.dot(attention, out_weight, preferred_element_type=jnp.float32)
    my_share = lax.psum_scatter(partial, "tp", scatter_dimension=1, tiled=True)
    power = lax.psum(jnp.sum(my_share * my_share, 1), "tp")
    inverse = lax.rsqrt(power / (share_width * tp_count) + EPSILON)
    normed = my_share * inverse[:, None]
    return (hidden.astype(jnp.float32) + normed * post_gain[None, :]).astype(jnp.bfloat16)


def solution(mesh):
    return jax.shard_map(
        body,
        mesh=mesh,
        in_specs=(
            P("req", "tp"),
            P("req", "tp"),
            P("req", "tp"),
            P("req", "tp"),
            P("tp"),
            P("tp"),
            P("tp", None),
            P("tp"),
            P(None, "req", None, "tp"),
            P(None, "req", None, "tp"),
            P("req", None, "tp"),
            P("req", None, "tp"),
            P("req"),
            P("req"),
            P(),
            P(),
        ),
        out_specs=P("req", "tp"),
        check_vma=False,
    )
```

```python
import jax
import jax.numpy as jnp
from jax import lax
from jax.sharding import PartitionSpec as P

HD = 128
SPAN = 288
DEC = 8


EPSILON = 1e-06
THETA = 500000.0
NEGATIVE = -1e30


def rotate(values, positions):
    half_width = values.shape[-1] // 2
    frequency = THETA ** (-(jnp.arange(half_width, dtype=jnp.float32) * 2.0 / values.shape[-1]))
    angles = positions.astype(jnp.float32)[:, None] * frequency[None, :]
    cosine = jnp.cos(angles)[:, None, :]
    sine_part = jnp.sin(angles)[:, None, :]
    first_half = values[..., :half_width]
    second = values[..., half_width:]
    return jnp.concatenate(
        [first_half * cosine - second * sine_part, second * cosine + first_half * sine_part], -1
    )


def softmax_part(scores, key_mask, values, form):
    masked = jnp.where(key_mask, scores, NEGATIVE)
    top_score = jnp.max(masked, -1)
    exp_terms = jnp.where(key_mask, jnp.exp(masked - top_score[..., None]), 0.0)
    weight_sum = jnp.sum(exp_terms, -1)
    numerator = jnp.einsum(
        form, exp_terms.astype(jnp.bfloat16), values, preferred_element_type=jnp.float32
    )
    return (top_score, weight_sum, numerator)


def merge_parts(top_scores, weight_sums, numerators):
    best_score = jnp.max(top_scores, 0)
    factor = jnp.exp(top_scores - best_score[None])
    weight_sum = jnp.sum(factor * weight_sums, 0)
    numerator = jnp.sum(factor[..., None] * numerators, 0)
    return numerator / weight_sum[..., None]


def body(
    hidden,
    raw_q,
    raw_k,
    raw_v,
    q_gain,
    k_gain,
    out_weight,
    post_gain,
    prefix_keys,
    prefix_values,
    key_cache,
    value_cache,
    slot_owner,
    slot_page,
    cache_lengths,
    span_offsets,
):
    groups = lax.axis_size("req")
    my_group = lax.axis_index("req")
    tp_count = lax.axis_size("tp")
    rows_group = SPAN + DEC
    local_width = raw_q.shape[1]
    local_heads = local_width // HD
    requests = groups * DEC
    score_scale = HD ** (-0.5)
    page_rows = key_cache.shape[1]


    own_lengths = lax.dynamic_slice_in_dim(cache_lengths, my_group * DEC, DEC)
    positions = jnp.concatenate(
        [span_offsets[my_group] + jnp.arange(SPAN, dtype=jnp.int32), own_lengths]
    )
    float_query = raw_q.astype(jnp.float32)
    float_key = raw_k.astype(jnp.float32)
    query_power, key_power = lax.psum(
        (jnp.sum(float_query * float_query, 1), jnp.sum(float_key * float_key, 1)), "tp"
    )
    full_width = local_width * tp_count
    normed_query = (
        float_query * lax.rsqrt(query_power / full_width + EPSILON)[:, None] * q_gain[None, :]
    )
    normed_key = float_key * lax.rsqrt(key_power / full_width + EPSILON)[:, None] * k_gain[None, :]
    query = rotate(normed_query.reshape(rows_group, local_heads, HD), positions).astype(
        jnp.bfloat16
    )
    key_rows = rotate(normed_key.reshape(rows_group, local_heads, HD), positions).astype(
        jnp.bfloat16
    )
    value_rows = raw_v.reshape(rows_group, local_heads, HD)

    pages_here = prefix_keys.shape[1]
    block_rows = pages_here * page_rows
    outgoing = jnp.concatenate(
        [
            prefix_keys.reshape(groups, block_rows, local_width),
            jnp.broadcast_to(
                query[None, SPAN:].reshape(1, DEC, local_width), (groups, DEC, local_width)
            ),
        ],
        1,
    )
    incoming = lax.all_to_all(outgoing, "req", split_axis=0, concat_axis=0, tiled=True)
    own_values = lax.all_to_all(
        prefix_values.reshape(groups, block_rows, local_width),
        "req",
        split_axis=0,
        concat_axis=0,
        tiled=True,
    )
    prefix_len = groups * block_rows
    own_keys = incoming[:, :block_rows].reshape(prefix_len, local_width)
    own_values = own_values.reshape(prefix_len, local_width)
    decode_queries = incoming[:, block_rows:].reshape(requests, local_heads, HD)
    live_slot = slot_owner >= 0
    owner_index = jnp.maximum(slot_owner, 0)
    slot_queries = decode_queries[owner_index]
    slot_keys = key_cache.reshape(key_cache.shape[0], page_rows, local_heads, HD)
    slot_values = value_cache.reshape(value_cache.shape[0], page_rows, local_heads, HD)
    scores = (
        jnp.einsum("shd,sphd->shp", slot_queries, slot_keys, preferred_element_type=jnp.float32)
        * score_scale
    )
    key_pos = slot_page[:, None] * page_rows + jnp.arange(page_rows, dtype=jnp.int32)[None, :]
    key_mask = live_slot[:, None] & (key_pos < cache_lengths[owner_index][:, None])
    top_score, weight_sum, numerator = softmax_part(
        scores, key_mask[:, None, :], slot_values, "shp,sphd->shd"
    )
    member = slot_owner[None, :] == jnp.arange(requests, dtype=jnp.int32)[:, None]
    best_score = jnp.max(jnp.where(member[:, :, None], top_score[None], NEGATIVE), 1)
    factor = jnp.where(member[:, :, None], jnp.exp(top_score[None] - best_score[:, None]), 0.0)
    request_total = jnp.einsum("rsh,sh->rh", factor, weight_sum, precision=lax.Precision.HIGHEST)
    request_numerator = jnp.einsum(
        "rsh,shd->rhd", factor, numerator, precision=lax.Precision.HIGHEST
    )
    packed = jnp.concatenate(
        [request_numerator, best_score[..., None], request_total[..., None]], -1
    )
    back = lax.all_to_all(packed, "req", split_axis=0, concat_axis=0, tiled=True)
    back = back.reshape(groups, DEC, local_heads, HD + 2)
    own_scores = (
        jnp.sum(query[SPAN:].astype(jnp.float32) * key_rows[SPAN:].astype(jnp.float32), -1)
        * score_scale
    )
    decode_out = merge_parts(
        jnp.concatenate([back[..., HD], own_scores[None]], 0),
        jnp.concatenate([back[..., HD + 1], jnp.ones_like(own_scores)[None]], 0),
        jnp.concatenate([back[..., :HD], value_rows[SPAN:].astype(jnp.float32)[None]], 0),
    )

    span_query = query[:SPAN].reshape(SPAN, local_width)
    span_keys = key_rows[:SPAN].reshape(SPAN, local_width)
    causal = jnp.arange(SPAN)[:, None] >= jnp.arange(SPAN)[None, :]
    prefix_mask = jnp.arange(prefix_len, dtype=jnp.int32) < span_offsets[my_group]
    head_outs = []
    for head in range(local_heads):
        cols = slice(head * HD, (head + 1) * HD)
        head_query = span_query[:, cols]
        pre_scores = (
            jnp.einsum(
                "qd,kd->qk", head_query, own_keys[:, cols], preferred_element_type=jnp.float32
            )
            * score_scale
        )
        self_scores = (
            jnp.einsum(
                "qd,kd->qk", head_query, span_keys[:, cols], preferred_element_type=jnp.float32
            )
            * score_scale
        )
        pre_masked = jnp.where(prefix_mask[None, :], pre_scores, NEGATIVE)
        self_masked = jnp.where(causal, self_scores, NEGATIVE)
        top = jnp.maximum(jnp.max(pre_masked, -1), jnp.max(self_masked, -1))
        pre_exp = jnp.where(prefix_mask[None, :], jnp.exp(pre_masked - top[:, None]), 0.0)
        self_exp = jnp.where(causal, jnp.exp(self_masked - top[:, None]), 0.0)
        total = jnp.sum(pre_exp, -1) + jnp.sum(self_exp, -1)
        head_numerator = jnp.dot(
            pre_exp.astype(jnp.bfloat16), own_values[:, cols], preferred_element_type=jnp.float32
        ) + jnp.dot(
            self_exp.astype(jnp.bfloat16), raw_v[:SPAN, cols], preferred_element_type=jnp.float32
        )
        head_outs.append(head_numerator / total[:, None])
    span_out = jnp.concatenate(head_outs, 1)

    merged = jnp.concatenate([span_out, decode_out.reshape(DEC, local_width)], 0)
    attention = merged.astype(jnp.bfloat16)
    share_width = post_gain.shape[0]
    partial = jnp.dot(attention, out_weight, preferred_element_type=jnp.float32)
    my_share = lax.psum_scatter(
        partial.astype(jnp.bfloat16), "tp", scatter_dimension=1, tiled=True
    ).astype(jnp.float32)
    power = lax.psum(jnp.sum(my_share * my_share, 1), "tp")
    inverse = lax.rsqrt(power / (share_width * tp_count) + EPSILON)
    normed = my_share * inverse[:, None]
    return (hidden.astype(jnp.float32) + normed * post_gain[None, :]).astype(jnp.bfloat16)


def solution(mesh):
    return jax.shard_map(
        body,
        mesh=mesh,
        in_specs=(
            P("req", "tp"),
            P("req", "tp"),
            P("req", "tp"),
            P("req", "tp"),
            P("tp"),
            P("tp"),
            P("tp", None),
            P("tp"),
            P(None, "req", None, "tp"),
            P(None, "req", None, "tp"),
            P("req", None, "tp"),
            P("req", None, "tp"),
            P("req"),
            P("req"),
            P(),
            P(),
        ),
        out_specs=P("req", "tp"),
        check_vma=False,
    )
```

```python
import jax
import jax.numpy as jnp
from jax import lax
from jax.sharding import PartitionSpec as P

HD = 128
SPAN = 288
DEC = 8


EPSILON = 1e-06
THETA = 500000.0
NEGATIVE = -1e30


def rotate(values, positions):
    half_width = values.shape[-1] // 2
    frequency = THETA ** (-(jnp.arange(half_width, dtype=jnp.float32) * 2.0 / values.shape[-1]))
    angles = positions.astype(jnp.float32)[:, None] * frequency[None, :]
    cosine = jnp.cos(angles)[:, None, :]
    sine_part = jnp.sin(angles)[:, None, :]
    first_half = values[..., :half_width]
    second = values[..., half_width:]
    return jnp.concatenate(
        [first_half * cosine - second * sine_part, second * cosine + first_half * sine_part], -1
    )


def softmax_part(scores, key_mask, values, form):
    masked = jnp.where(key_mask, scores, NEGATIVE)
    top_score = jnp.max(masked, -1)
    exp_terms = jnp.where(key_mask, jnp.exp(masked - top_score[..., None]), 0.0)
    weight_sum = jnp.sum(exp_terms, -1)
    numerator = jnp.einsum(
        form, exp_terms.astype(jnp.bfloat16), values, preferred_element_type=jnp.float32
    )
    return (top_score, weight_sum, numerator)


def merge_parts(top_scores, weight_sums, numerators):
    best_score = jnp.max(top_scores, 0)
    factor = jnp.exp(top_scores - best_score[None])
    weight_sum = jnp.sum(factor * weight_sums, 0)
    numerator = jnp.sum(factor[..., None] * numerators, 0)
    return numerator / weight_sum[..., None]


def body(
    hidden,
    raw_q,
    raw_k,
    raw_v,
    q_gain,
    k_gain,
    out_weight,
    post_gain,
    prefix_keys,
    prefix_values,
    key_cache,
    value_cache,
    slot_owner,
    slot_page,
    cache_lengths,
    span_offsets,
):
    groups = lax.axis_size("req")
    my_group = lax.axis_index("req")
    tp_count = lax.axis_size("tp")
    rows_group = SPAN + DEC
    local_width = raw_q.shape[1]
    local_heads = local_width // HD
    requests = groups * DEC
    score_scale = HD ** (-0.5)
    page_rows = key_cache.shape[1]


    own_lengths = lax.dynamic_slice_in_dim(cache_lengths, my_group * DEC, DEC)
    positions = jnp.concatenate(
        [span_offsets[my_group] + jnp.arange(SPAN, dtype=jnp.int32), own_lengths]
    )
    float_query = raw_q.astype(jnp.float32)
    float_key = raw_k.astype(jnp.float32)
    query_power, key_power = lax.psum(
        (jnp.sum(float_query * float_query, 1), jnp.sum(float_key * float_key, 1)), "tp"
    )
    full_width = local_width * tp_count
    normed_query = (
        float_query * lax.rsqrt(query_power / full_width + EPSILON)[:, None] * q_gain[None, :]
    )
    normed_key = float_key * lax.rsqrt(key_power / full_width + EPSILON)[:, None] * k_gain[None, :]
    query = rotate(normed_query.reshape(rows_group, local_heads, HD), positions).astype(
        jnp.bfloat16
    )
    key_rows = rotate(normed_key.reshape(rows_group, local_heads, HD), positions).astype(
        jnp.bfloat16
    )
    value_rows = raw_v.reshape(rows_group, local_heads, HD)

    pages_here = prefix_keys.shape[1]
    block_rows = pages_here * page_rows
    half_rows = page_rows // 2
    key_pages = prefix_keys.reshape(groups, block_rows, local_width)
    outgoing = jnp.concatenate(
        [
            key_pages[:, :half_rows],
            jnp.broadcast_to(
                query[None, SPAN:].reshape(1, DEC, local_width), (groups, DEC, local_width)
            ),
        ],
        1,
    )
    incoming = lax.all_to_all(outgoing, "req", split_axis=0, concat_axis=0, tiled=True)
    own_values = lax.all_to_all(
        prefix_values.reshape(groups, block_rows, local_width),
        "req",
        split_axis=0,
        concat_axis=0,
        tiled=True,
    )
    key_rest = lax.all_to_all(
        key_pages[:, half_rows:], "req", split_axis=0, concat_axis=0, tiled=True
    )
    half_len = groups * half_rows
    keys_front = incoming[:, :half_rows].reshape(half_len, local_width)
    keys_back = key_rest.reshape(half_len, local_width)
    values_grid = own_values.reshape(groups, block_rows, local_width)
    values_front = values_grid[:, :half_rows].reshape(half_len, local_width)
    values_back = values_grid[:, half_rows:].reshape(half_len, local_width)
    decode_queries = incoming[:, half_rows:].reshape(requests, local_heads, HD)
    live_slot = slot_owner >= 0
    owner_index = jnp.maximum(slot_owner, 0)
    slot_queries = decode_queries[owner_index]
    slot_keys = key_cache.reshape(key_cache.shape[0], page_rows, local_heads, HD)
    slot_values = value_cache.reshape(value_cache.shape[0], page_rows, local_heads, HD)
    scores = (
        jnp.einsum("shd,sphd->shp", slot_queries, slot_keys, preferred_element_type=jnp.float32)
        * score_scale
    )
    key_pos = slot_page[:, None] * page_rows + jnp.arange(page_rows, dtype=jnp.int32)[None, :]
    key_mask = live_slot[:, None] & (key_pos < cache_lengths[owner_index][:, None])
    top_score, weight_sum, numerator = softmax_part(
        scores, key_mask[:, None, :], slot_values, "shp,sphd->shd"
    )
    member = slot_owner[None, :] == jnp.arange(requests, dtype=jnp.int32)[:, None]
    best_score = jnp.max(jnp.where(member[:, :, None], top_score[None], NEGATIVE), 1)
    factor = jnp.where(member[:, :, None], jnp.exp(top_score[None] - best_score[:, None]), 0.0)
    request_total = jnp.einsum("rsh,sh->rh", factor, weight_sum, precision=lax.Precision.HIGHEST)
    request_numerator = jnp.einsum(
        "rsh,shd->rhd", factor, numerator, precision=lax.Precision.HIGHEST
    )
    packed = jnp.concatenate(
        [request_numerator, best_score[..., None], request_total[..., None]], -1
    )
    back = lax.all_to_all(packed, "req", split_axis=0, concat_axis=0, tiled=True)
    back = back.reshape(groups, DEC, local_heads, HD + 2)
    own_scores = (
        jnp.sum(query[SPAN:].astype(jnp.float32) * key_rows[SPAN:].astype(jnp.float32), -1)
        * score_scale
    )
    decode_out = merge_parts(
        jnp.concatenate([back[..., HD], own_scores[None]], 0),
        jnp.concatenate([back[..., HD + 1], jnp.ones_like(own_scores)[None]], 0),
        jnp.concatenate([back[..., :HD], value_rows[SPAN:].astype(jnp.float32)[None]], 0),
    )

    span_query = query[:SPAN].reshape(SPAN, local_width)
    span_keys = key_rows[:SPAN].reshape(SPAN, local_width)
    causal = jnp.arange(SPAN)[:, None] >= jnp.arange(SPAN)[None, :]
    row_in_page = jnp.arange(half_rows, dtype=jnp.int32)[None, :]
    page_start = jnp.arange(groups, dtype=jnp.int32)[:, None] * page_rows
    front_mask = (page_start + row_in_page).reshape(-1) < span_offsets[my_group]
    back_mask = (page_start + half_rows + row_in_page).reshape(-1) < span_offsets[my_group]
    head_outs = []
    for head in range(local_heads):
        cols = slice(head * HD, (head + 1) * HD)
        head_query = span_query[:, cols]
        front_scores = (
            jnp.einsum(
                "qd,kd->qk", head_query, keys_front[:, cols], preferred_element_type=jnp.float32
            )
            * score_scale
        )
        front_masked = jnp.where(front_mask[None, :], front_scores, NEGATIVE)
        front_top = jnp.max(front_masked, -1)
        front_exp = jnp.where(
            front_mask[None, :], jnp.exp(front_masked - front_top[:, None]), 0.0
        )
        front_total = jnp.sum(front_exp, -1)
        front_numerator = jnp.dot(
            front_exp.astype(jnp.bfloat16), values_front[:, cols], preferred_element_type=jnp.float32
        )
        back_scores = (
            jnp.einsum(
                "qd,kd->qk", head_query, keys_back[:, cols], preferred_element_type=jnp.float32
            )
            * score_scale
        )
        self_scores = (
            jnp.einsum(
                "qd,kd->qk", head_query, span_keys[:, cols], preferred_element_type=jnp.float32
            )
            * score_scale
        )
        back_masked = jnp.where(back_mask[None, :], back_scores, NEGATIVE)
        self_masked = jnp.where(causal, self_scores, NEGATIVE)
        back_top = jnp.maximum(jnp.max(back_masked, -1), jnp.max(self_masked, -1))
        back_exp = jnp.where(back_mask[None, :], jnp.exp(back_masked - back_top[:, None]), 0.0)
        self_exp = jnp.where(causal, jnp.exp(self_masked - back_top[:, None]), 0.0)
        back_total = jnp.sum(back_exp, -1) + jnp.sum(self_exp, -1)
        back_numerator = jnp.dot(
            back_exp.astype(jnp.bfloat16), values_back[:, cols], preferred_element_type=jnp.float32
        ) + jnp.dot(
            self_exp.astype(jnp.bfloat16), raw_v[:SPAN, cols], preferred_element_type=jnp.float32
        )
        top = jnp.maximum(front_top, back_top)
        front_factor = jnp.exp(front_top - top)
        back_factor = jnp.exp(back_top - top)
        total = front_factor * front_total + back_factor * back_total
        head_numerator = (
            front_factor[:, None] * front_numerator + back_factor[:, None] * back_numerator
        )
        head_outs.append(head_numerator / total[:, None])
    span_out = jnp.concatenate(head_outs, 1)

    merged = jnp.concatenate([span_out, decode_out.reshape(DEC, local_width)], 0)
    attention = merged.astype(jnp.bfloat16)
    share_width = post_gain.shape[0]
    partial = jnp.dot(attention, out_weight, preferred_element_type=jnp.float32)
    my_share = lax.psum_scatter(partial, "tp", scatter_dimension=1, tiled=True)
    power = lax.psum(jnp.sum(my_share * my_share, 1), "tp")
    inverse = lax.rsqrt(power / (share_width * tp_count) + EPSILON)
    normed = my_share * inverse[:, None]
    return (hidden.astype(jnp.float32) + normed * post_gain[None, :]).astype(jnp.bfloat16)


def solution(mesh):
    return jax.shard_map(
        body,
        mesh=mesh,
        in_specs=(
            P("req", "tp"),
            P("req", "tp"),
            P("req", "tp"),
            P("req", "tp"),
            P("tp"),
            P("tp"),
            P("tp", None),
            P("tp"),
            P(None, "req", None, "tp"),
            P(None, "req", None, "tp"),
            P("req", None, "tp"),
            P("req", None, "tp"),
            P("req"),
            P("req"),
            P(),
            P(),
        ),
        out_specs=P("req", "tp"),
        check_vma=False,
    )
```

```python
import jax
import jax.numpy as jnp
from jax import lax
from jax.sharding import PartitionSpec as P

HD = 128
SPAN = 288
DEC = 8


EPSILON = 1e-06
THETA = 500000.0
NEGATIVE = -1e30


def rotate(values, positions):
    half_width = values.shape[-1] // 2
    frequency = THETA ** (-(jnp.arange(half_width, dtype=jnp.float32) * 2.0 / values.shape[-1]))
    angles = positions.astype(jnp.float32)[:, None] * frequency[None, :]
    cosine = jnp.cos(angles)[:, None, :]
    sine_part = jnp.sin(angles)[:, None, :]
    first_half = values[..., :half_width]
    second = values[..., half_width:]
    return jnp.concatenate(
        [first_half * cosine - second * sine_part, second * cosine + first_half * sine_part], -1
    )


def softmax_part(scores, key_mask, values, form):
    masked = jnp.where(key_mask, scores, NEGATIVE)
    top_score = jnp.max(masked, -1)
    exp_terms = jnp.where(key_mask, jnp.exp(masked - top_score[..., None]), 0.0)
    weight_sum = jnp.sum(exp_terms, -1)
    numerator = jnp.einsum(
        form, exp_terms.astype(jnp.bfloat16), values, preferred_element_type=jnp.float32
    )
    return (top_score, weight_sum, numerator)


def merge_parts(top_scores, weight_sums, numerators):
    best_score = jnp.max(top_scores, 0)
    factor = jnp.exp(top_scores - best_score[None])
    weight_sum = jnp.sum(factor * weight_sums, 0)
    numerator = jnp.sum(factor[..., None] * numerators, 0)
    return numerator / weight_sum[..., None]


def body(
    hidden,
    raw_q,
    raw_k,
    raw_v,
    q_gain,
    k_gain,
    out_weight,
    post_gain,
    prefix_keys,
    prefix_values,
    key_cache,
    value_cache,
    slot_owner,
    slot_page,
    cache_lengths,
    span_offsets,
):
    groups = lax.axis_size("req")
    my_group = lax.axis_index("req")
    tp_count = lax.axis_size("tp")
    rows_group = SPAN + DEC
    local_width = raw_q.shape[1]
    local_heads = local_width // HD
    requests = groups * DEC
    score_scale = HD ** (-0.5)
    page_rows = key_cache.shape[1]


    own_lengths = lax.dynamic_slice_in_dim(cache_lengths, my_group * DEC, DEC)
    positions = jnp.concatenate(
        [span_offsets[my_group] + jnp.arange(SPAN, dtype=jnp.int32), own_lengths]
    )
    float_query = raw_q.astype(jnp.float32)
    float_key = raw_k.astype(jnp.float32)
    query_power, key_power = lax.psum(
        (jnp.sum(float_query * float_query, 1), jnp.sum(float_key * float_key, 1)), "tp"
    )
    full_width = local_width * tp_count
    normed_query = (
        float_query * lax.rsqrt(query_power / full_width + EPSILON)[:, None] * q_gain[None, :]
    )
    normed_key = float_key * lax.rsqrt(key_power / full_width + EPSILON)[:, None] * k_gain[None, :]
    query = rotate(normed_query.reshape(rows_group, local_heads, HD), positions).astype(
        jnp.bfloat16
    )
    key_rows = rotate(normed_key.reshape(rows_group, local_heads, HD), positions).astype(
        jnp.bfloat16
    )
    value_rows = raw_v.reshape(rows_group, local_heads, HD)

    pages_here = prefix_keys.shape[1]
    block_rows = pages_here * page_rows
    outgoing = jnp.concatenate(
        [
            prefix_keys.reshape(groups, block_rows, local_width),
            jnp.broadcast_to(
                query[None, SPAN:].reshape(1, DEC, local_width), (groups, DEC, local_width)
            ),
        ],
        1,
    )
    incoming = lax.all_to_all(outgoing, "req", split_axis=0, concat_axis=0, tiled=True)
    own_values = lax.all_to_all(
        prefix_values.reshape(groups, block_rows, local_width),
        "req",
        split_axis=0,
        concat_axis=0,
        tiled=True,
    )
    prefix_len = groups * block_rows
    own_keys = incoming[:, :block_rows].reshape(prefix_len, local_width)
    own_values = own_values.reshape(prefix_len, local_width)
    decode_queries = incoming[:, block_rows:].reshape(requests, local_heads, HD)
    live_slot = slot_owner >= 0
    owner_index = jnp.maximum(slot_owner, 0)
    slot_queries = decode_queries[owner_index]
    slot_keys = key_cache.reshape(key_cache.shape[0], page_rows, local_heads, HD)
    slot_values = value_cache.reshape(value_cache.shape[0], page_rows, local_heads, HD)
    scores = (
        jnp.einsum("shd,sphd->shp", slot_queries, slot_keys, preferred_element_type=jnp.float32)
        * score_scale
    )
    key_pos = slot_page[:, None] * page_rows + jnp.arange(page_rows, dtype=jnp.int32)[None, :]
    key_mask = live_slot[:, None] & (key_pos < cache_lengths[owner_index][:, None])
    top_score, weight_sum, numerator = softmax_part(
        scores, key_mask[:, None, :], slot_values, "shp,sphd->shd"
    )
    member = slot_owner[None, :] == jnp.arange(requests, dtype=jnp.int32)[:, None]
    best_score = jnp.max(jnp.where(member[:, :, None], top_score[None], NEGATIVE), 1)
    factor = jnp.where(member[:, :, None], jnp.exp(top_score[None] - best_score[:, None]), 0.0)
    request_total = jnp.einsum("rsh,sh->rh", factor, weight_sum, precision=lax.Precision.HIGHEST)
    request_numerator = jnp.einsum(
        "rsh,shd->rhd", factor, numerator, precision=lax.Precision.HIGHEST
    )
    packed = jnp.concatenate(
        [request_numerator, best_score[..., None], request_total[..., None]], -1
    )
    back = lax.all_to_all(packed, "req", split_axis=0, concat_axis=0, tiled=True)
    back = back.reshape(groups, DEC, local_heads, HD + 2)
    own_scores = (
        jnp.sum(query[SPAN:].astype(jnp.float32) * key_rows[SPAN:].astype(jnp.float32), -1)
        * score_scale
    )
    decode_out = merge_parts(
        jnp.concatenate([back[..., HD], own_scores[None]], 0),
        jnp.concatenate([back[..., HD + 1], jnp.ones_like(own_scores)[None]], 0),
        jnp.concatenate([back[..., :HD], value_rows[SPAN:].astype(jnp.float32)[None]], 0),
    )

    span_query = query[:SPAN].reshape(SPAN, local_width)
    span_keys = key_rows[:SPAN].reshape(SPAN, local_width)
    causal = jnp.arange(SPAN)[:, None] >= jnp.arange(SPAN)[None, :]
    prefix_mask = jnp.arange(prefix_len, dtype=jnp.int32) < span_offsets[my_group]
    head_outs = []
    for head in range(local_heads):
        cols = slice(head * HD, (head + 1) * HD)
        head_query = span_query[:, cols]
        pre_scores = (
            jnp.einsum(
                "qd,kd->qk", head_query, own_keys[:, cols], preferred_element_type=jnp.float32
            )
            * score_scale
        )
        self_scores = (
            jnp.einsum(
                "qd,kd->qk", head_query, span_keys[:, cols], preferred_element_type=jnp.float32
            )
            * score_scale
        )
        pre_masked = jnp.where(prefix_mask[None, :], pre_scores, NEGATIVE)
        self_masked = jnp.where(causal, self_scores, NEGATIVE)
        top = jnp.maximum(jnp.max(pre_masked, -1), jnp.max(self_masked, -1))
        pre_exp = jnp.where(prefix_mask[None, :], jnp.exp(pre_masked - top[:, None]), 0.0)
        self_exp = jnp.where(causal, jnp.exp(self_masked - top[:, None]), 0.0)
        total = jnp.sum(pre_exp, -1) + jnp.sum(self_exp, -1)
        head_numerator = jnp.dot(
            pre_exp.astype(jnp.bfloat16), own_values[:, cols], preferred_element_type=jnp.float32
        ) + jnp.dot(
            self_exp.astype(jnp.bfloat16), raw_v[:SPAN, cols], preferred_element_type=jnp.float32
        )
        head_outs.append(head_numerator / total[:, None])
    span_out = jnp.concatenate(head_outs, 1)

    merged = jnp.concatenate([span_out, decode_out.reshape(DEC, local_width)], 0)
    attention = merged.astype(jnp.bfloat16)
    share_width = post_gain.shape[0]
    column_blocks = out_weight.reshape(local_width, tp_count, share_width)
    partial = jnp.einsum(
        "rk,kcn->crn", attention, column_blocks, preferred_element_type=jnp.float32
    )
    pieces = lax.all_to_all(
        partial.astype(jnp.bfloat16), "tp", split_axis=0, concat_axis=0, tiled=True
    )
    my_share = jnp.sum(pieces.astype(jnp.float32), 0)
    power = lax.psum(jnp.sum(my_share * my_share, 1), "tp")
    inverse = lax.rsqrt(power / (share_width * tp_count) + EPSILON)
    normed = my_share * inverse[:, None]
    return (hidden.astype(jnp.float32) + normed * post_gain[None, :]).astype(jnp.bfloat16)


def solution(mesh):
    return jax.shard_map(
        body,
        mesh=mesh,
        in_specs=(
            P("req", "tp"),
            P("req", "tp"),
            P("req", "tp"),
            P("req", "tp"),
            P("tp"),
            P("tp"),
            P("tp", None),
            P("tp"),
            P(None, "req", None, "tp"),
            P(None, "req", None, "tp"),
            P("req", None, "tp"),
            P("req", None, "tp"),
            P("req"),
            P("req"),
            P(),
            P(),
        ),
        out_specs=P("req", "tp"),
        check_vma=False,
    )
```

```python
import jax
import jax.numpy as jnp
from jax import lax
from jax.sharding import PartitionSpec as P

HD = 128
SPAN = 288
DEC = 8


EPSILON = 1e-06
THETA = 500000.0
NEGATIVE = -1e30


def rotate(values, positions):
    half_width = values.shape[-1] // 2
    frequency = THETA ** (-(jnp.arange(half_width, dtype=jnp.float32) * 2.0 / values.shape[-1]))
    angles = positions.astype(jnp.float32)[:, None] * frequency[None, :]
    cosine = jnp.cos(angles)[:, None, :]
    sine_part = jnp.sin(angles)[:, None, :]
    first_half = values[..., :half_width]
    second = values[..., half_width:]
    return jnp.concatenate(
        [first_half * cosine - second * sine_part, second * cosine + first_half * sine_part], -1
    )


def softmax_part(scores, key_mask, values, form):
    masked = jnp.where(key_mask, scores, NEGATIVE)
    top_score = jnp.max(masked, -1)
    exp_terms = jnp.where(key_mask, jnp.exp(masked - top_score[..., None]), 0.0)
    weight_sum = jnp.sum(exp_terms, -1)
    numerator = jnp.einsum(
        form, exp_terms.astype(jnp.bfloat16), values, preferred_element_type=jnp.float32
    )
    return (top_score, weight_sum, numerator)


def merge_parts(top_scores, weight_sums, numerators):
    best_score = jnp.max(top_scores, 0)
    factor = jnp.exp(top_scores - best_score[None])
    weight_sum = jnp.sum(factor * weight_sums, 0)
    numerator = jnp.sum(factor[..., None] * numerators, 0)
    return numerator / weight_sum[..., None]


def body(
    hidden,
    raw_q,
    raw_k,
    raw_v,
    q_gain,
    k_gain,
    out_weight,
    post_gain,
    prefix_keys,
    prefix_values,
    key_cache,
    value_cache,
    slot_owner,
    slot_page,
    cache_lengths,
    span_offsets,
):
    groups = lax.axis_size("req")
    my_group = lax.axis_index("req")
    tp_count = lax.axis_size("tp")
    rows_group = SPAN + DEC
    local_width = raw_q.shape[1]
    local_heads = local_width // HD
    requests = groups * DEC
    score_scale = HD ** (-0.5)
    page_rows = key_cache.shape[1]


    own_lengths = lax.dynamic_slice_in_dim(cache_lengths, my_group * DEC, DEC)
    positions = jnp.concatenate(
        [span_offsets[my_group] + jnp.arange(SPAN, dtype=jnp.int32), own_lengths]
    )
    float_query = raw_q.astype(jnp.float32)
    float_key = raw_k.astype(jnp.float32)
    query_power, key_power = lax.psum(
        (jnp.sum(float_query * float_query, 1), jnp.sum(float_key * float_key, 1)), "tp"
    )
    full_width = local_width * tp_count
    normed_query = (
        float_query * lax.rsqrt(query_power / full_width + EPSILON)[:, None] * q_gain[None, :]
    )
    normed_key = float_key * lax.rsqrt(key_power / full_width + EPSILON)[:, None] * k_gain[None, :]
    query = rotate(normed_query.reshape(rows_group, local_heads, HD), positions).astype(
        jnp.bfloat16
    )
    key_rows = rotate(normed_key.reshape(rows_group, local_heads, HD), positions).astype(
        jnp.bfloat16
    )
    value_rows = raw_v.reshape(rows_group, local_heads, HD)

    pages_here = prefix_keys.shape[1]
    block_rows = pages_here * page_rows
    outgoing = jnp.concatenate(
        [
            prefix_keys.reshape(groups, block_rows, local_width),
            jnp.broadcast_to(
                query[None, SPAN:].reshape(1, DEC, local_width), (groups, DEC, local_width)
            ),
        ],
        1,
    )
    incoming = lax.all_to_all(outgoing, "req", split_axis=0, concat_axis=0, tiled=True)
    own_values = lax.all_to_all(
        prefix_values.reshape(groups, block_rows, local_width),
        "req",
        split_axis=0,
        concat_axis=0,
        tiled=True,
    )
    prefix_len = groups * block_rows
    own_keys = incoming[:, :block_rows].reshape(prefix_len, local_width)
    own_values = own_values.reshape(prefix_len, local_width)
    decode_queries = incoming[:, block_rows:].reshape(requests, local_heads, HD)
    live_slot = slot_owner >= 0
    owner_index = jnp.maximum(slot_owner, 0)
    slot_queries = decode_queries[owner_index]
    slot_keys = key_cache.reshape(key_cache.shape[0], page_rows, local_heads, HD)
    slot_values = value_cache.reshape(value_cache.shape[0], page_rows, local_heads, HD)
    scores = (
        jnp.einsum("shd,sphd->shp", slot_queries, slot_keys, preferred_element_type=jnp.float32)
        * score_scale
    )
    key_pos = slot_page[:, None] * page_rows + jnp.arange(page_rows, dtype=jnp.int32)[None, :]
    key_mask = live_slot[:, None] & (key_pos < cache_lengths[owner_index][:, None])
    top_score, weight_sum, numerator = softmax_part(
        scores, key_mask[:, None, :], slot_values, "shp,sphd->shd"
    )
    member = slot_owner[None, :] == jnp.arange(requests, dtype=jnp.int32)[:, None]
    best_score = jnp.max(jnp.where(member[:, :, None], top_score[None], NEGATIVE), 1)
    factor = jnp.where(member[:, :, None], jnp.exp(top_score[None] - best_score[:, None]), 0.0)
    request_total = jnp.einsum("rsh,sh->rh", factor, weight_sum, precision=lax.Precision.HIGHEST)
    request_numerator = jnp.einsum(
        "rsh,shd->rhd", factor, numerator, precision=lax.Precision.HIGHEST
    )
    packed = jnp.concatenate(
        [request_numerator, best_score[..., None], request_total[..., None]], -1
    )
    back = lax.all_to_all(packed, "req", split_axis=0, concat_axis=0, tiled=True)
    back = back.reshape(groups, DEC, local_heads, HD + 2)
    own_scores = (
        jnp.sum(query[SPAN:].astype(jnp.float32) * key_rows[SPAN:].astype(jnp.float32), -1)
        * score_scale
    )
    decode_out = merge_parts(
        jnp.concatenate([back[..., HD], own_scores[None]], 0),
        jnp.concatenate([back[..., HD + 1], jnp.ones_like(own_scores)[None]], 0),
        jnp.concatenate([back[..., :HD], value_rows[SPAN:].astype(jnp.float32)[None]], 0),
    )

    span_query = query[:SPAN].reshape(SPAN, local_width)
    span_keys = key_rows[:SPAN].reshape(SPAN, local_width)
    causal = jnp.arange(SPAN)[:, None] >= jnp.arange(SPAN)[None, :]
    prefix_mask = jnp.arange(prefix_len, dtype=jnp.int32) < span_offsets[my_group]
    head_outs = []
    for head in range(local_heads):
        cols = slice(head * HD, (head + 1) * HD)
        head_query = span_query[:, cols]
        pre_scores = (
            jnp.einsum(
                "qd,kd->qk", head_query, own_keys[:, cols], preferred_element_type=jnp.float32
            )
            * score_scale
        )
        self_scores = (
            jnp.einsum(
                "qd,kd->qk", head_query, span_keys[:, cols], preferred_element_type=jnp.float32
            )
            * score_scale
        )
        pre_masked = jnp.where(prefix_mask[None, :], pre_scores, NEGATIVE)
        self_masked = jnp.where(causal, self_scores, NEGATIVE)
        top = jnp.maximum(jnp.max(pre_masked, -1), jnp.max(self_masked, -1))
        pre_exp = jnp.where(prefix_mask[None, :], jnp.exp(pre_masked - top[:, None]), 0.0)
        self_exp = jnp.where(causal, jnp.exp(self_masked - top[:, None]), 0.0)
        total = jnp.sum(pre_exp, -1) + jnp.sum(self_exp, -1)
        head_numerator = jnp.dot(
            pre_exp.astype(jnp.bfloat16), own_values[:, cols], preferred_element_type=jnp.float32
        ) + jnp.dot(
            self_exp.astype(jnp.bfloat16), raw_v[:SPAN, cols], preferred_element_type=jnp.float32
        )
        head_outs.append(head_numerator / total[:, None])
    span_out = jnp.concatenate(head_outs, 1)

    merged = jnp.concatenate([span_out, decode_out.reshape(DEC, local_width)], 0)
    attention = merged.astype(jnp.bfloat16)
    share_width = post_gain.shape[0]
    column_blocks = out_weight.reshape(local_width, tp_count, share_width)
    partial = jnp.einsum(
        "rk,kcn->crn", attention, column_blocks, preferred_element_type=jnp.float32
    )
    pieces = lax.all_to_all(
        partial.astype(jnp.bfloat16), "tp", split_axis=0, concat_axis=0, tiled=True
    )
    my_share = jnp.sum(pieces.astype(jnp.float32), 0)
    power_part = jnp.sum(my_share * my_share, 1)
    power_copies = jnp.broadcast_to(power_part[None], (tp_count, power_part.shape[0]))
    power = jnp.sum(
        lax.all_to_all(power_copies, "tp", split_axis=0, concat_axis=0, tiled=True), 0
    )
    inverse = lax.rsqrt(power / (share_width * tp_count) + EPSILON)
    normed = my_share * inverse[:, None]
    return (hidden.astype(jnp.float32) + normed * post_gain[None, :]).astype(jnp.bfloat16)


def solution(mesh):
    return jax.shard_map(
        body,
        mesh=mesh,
        in_specs=(
            P("req", "tp"),
            P("req", "tp"),
            P("req", "tp"),
            P("req", "tp"),
            P("tp"),
            P("tp"),
            P("tp", None),
            P("tp"),
            P(None, "req", None, "tp"),
            P(None, "req", None, "tp"),
            P("req", None, "tp"),
            P("req", None, "tp"),
            P("req"),
            P("req"),
            P(),
            P(),
        ),
        out_specs=P("req", "tp"),
        check_vma=False,
    )
```
